32 devices in a mesh: req: 8 (over z, y), seq: 4 (over x, core).
Axes of the slice: x: 2, y: 2, z: 4, core: 2. Of those that a mesh axis runs over, the one named last changes fastest.
Arguments:
- prompt_query: bfloat16 [8, 4096, 1024], P('req', 'seq'), may hold values from -6 to 6
- prompt_key: bfloat16 [8, 4096, 1024], P('req', 'seq'), may hold values from -6 to 6
- prompt_value: bfloat16 [8, 4096, 2048], P('req', 'seq'), may hold values from -6 to 6
- prompt_gate_logit: bfloat16 [8, 4096, 1024], P('req', 'seq'), may hold values from -12 to 12
- prompt_out_gate: bfloat16 [8, 4096, 2048], P('req', 'seq'), may hold values from -6 to 6
- prompt_len: int32 [8], P('req'), may hold values from 1024 to 4096, as said below
- suffix_query: bfloat16 [32, 256, 1024], P('req'), may hold values from -6 to 6
- suffix_key: bfloat16 [32, 256, 1024], P('req'), may hold values from -6 to 6
- suffix_value: bfloat16 [32, 256, 2048], P('req', None, 'seq'), may hold values from -6 to 6
- suffix_gate_logit: bfloat16 [32, 256, 1024], P('req'), may hold values from -12 to 12
- suffix_out_gate: bfloat16 [32, 256, 2048], P('req', None, 'seq'), may hold values from -6 to 6
- suffix_len: int32 [32], P('req'), may hold values from 64 to 256, as said below
- request_group: int32 [32], P('req'), may hold values from 0 to 7, as said below
- norm_gain: float32 [512], replicated, may hold values from 0.1 to 1.9
Outputs:
- prompt_out: bfloat16 [8, 4096, 2048], P('req', 'seq')
- suffix_out: bfloat16 [32, 256, 2048], P('req', None, 'seq')
The draws below stay inside these ranges and needn't reach their ends.
Inputs may be any that keep to these rules, and one draw needn't show every extreme that they name: `prompt_len`: some group's prompt fills all 4096 positions. `suffix_len`: some request's suffix fills all 256 positions. `request_group`: every group has at least one request.
All inputs are finite; a program needn't handle non-finite values.
Results may differ from the reference program's by a relative error of at most 0.001.
Values sent between devices are 32-bit elements; how exact they have to be, the bound alone decides.
A program may use at most 192 MiB of HBM per device.

```python
import jax
import jax.numpy as jnp
from jax import lax

HEAD_COUNT = 4
KEY_CHANNELS = 256
DVH = 512
BL = 64
SUFMAX = 256
GROUPS = 8
PROMPT = 4096
REQS = 32


def channel_lives(key):
    pick_key, fast_key, slow_key = jax.random.split(jax.random.fold_in(key, 11), 3)
    fast_share = 0.5
    chain_length = float(PROMPT + SUFMAX)
    fast_mask = jax.random.uniform(pick_key, (HEAD_COUNT * KEY_CHANNELS,)) < fast_share
    fast_life = jnp.exp(jax.random.uniform(fast_key, (HEAD_COUNT * KEY_CHANNELS,), minval=jnp.log(30.0), maxval=jnp.log(50.0)))
    slow_life = jnp.exp(jax.random.uniform(slow_key, (HEAD_COUNT * KEY_CHANNELS,), minval=jnp.log(2.0 * chain_length), maxval=jnp.log(8.0 * chain_length)))
    return jnp.where(fast_mask, fast_life, slow_life)


def gate_preactivation(key, seed_offset, number_of_rows, token_positions, spike_count):
    channel_life = channel_lives(key)
    block_random_key, noise_random_key, location_random_key, spike_random_key = jax.random.split(jax.random.fold_in(key, seed_offset), 4)
    factor = jnp.exp(jax.random.uniform(block_random_key, (number_of_rows, token_positions // BL, HEAD_COUNT * KEY_CHANNELS), minval=jnp.log(0.7), maxval=jnp.log(1.4)))
    factor = jnp.repeat(factor, BL, axis=1)
    jitter_factor = jax.random.uniform(noise_random_key, (number_of_rows, token_positions, HEAD_COUNT * KEY_CHANNELS), minval=0.5, maxval=1.5)
    per_step_rates = factor * jitter_factor / channel_life[None, None, :]
    spike_places = jax.random.randint(location_random_key, (number_of_rows, spike_count), 0, token_positions)
    spike_flag = jnp.any(jnp.arange(token_positions)[None, :, None] == spike_places[:, None, :], axis=-1)
    retained_fraction = jax.random.uniform(spike_random_key, (number_of_rows, token_positions, HEAD_COUNT * KEY_CHANNELS), minval=0.6, maxval=0.8)
    per_step_rates = jnp.where(spike_flag[:, :, None], -jnp.log(retained_fraction), per_step_rates)
    logits = -jnp.log(jnp.expm1(16.0 * per_step_rates))
    return logits.astype(jnp.bfloat16)


def draw_prompt_gate_logit(key, part):
    return gate_preactivation(key, 1, GROUPS, PROMPT, 2)


def draw_suffix_gate_logit(key, part):
    return gate_preactivation(key, 2, REQS, SUFMAX, 1)


def draw_prompt_len(key, part):
    lengths_key, longest_key = jax.random.split(jax.random.fold_in(key, 21))
    lengths = jax.random.randint(lengths_key, (GROUPS,), PROMPT // 4, PROMPT + 1)
    longest = jax.random.randint(longest_key, (), 0, GROUPS)
    return jnp.where(jnp.arange(GROUPS) == longest, PROMPT, lengths).astype(jnp.int32)


def draw_suffix_len(key, part):
    lengths_key, longest_key = jax.random.split(jax.random.fold_in(key, 22))
    lengths = jax.random.randint(lengths_key, (REQS,), SUFMAX // 4, SUFMAX + 1)
    longest = jax.random.randint(longest_key, (), 0, REQS)
    return jnp.where(jnp.arange(REQS) == longest, SUFMAX, lengths).astype(jnp.int32)


def draw_request_group(key, part):
    extra_key, order_key = jax.random.split(jax.random.fold_in(key, 23))
    extra_members = jax.random.randint(extra_key, (REQS - GROUPS,), 0, GROUPS).astype(jnp.int32)
    members = jnp.concatenate([jnp.arange(GROUPS, dtype=jnp.int32), extra_members])
    return jax.random.permutation(order_key, members).astype(jnp.int32)


def steps_of(stream_key, dims, pieces, smallest, high):
    def one(axis_at, blocks):
        steps = jax.random.uniform(jax.random.fold_in(jax.random.fold_in(stream_key, 6), axis_at), (blocks,), jnp.float32, smallest / len(pieces), high / len(pieces))
        return jnp.repeat(jnp.exp(steps), dims[axis_at] // blocks).reshape((-1,) + (1,) * (len(dims) - axis_at - 1))

    loudness = one(*pieces[0])
    for cut in pieces[1:]:
        loudness = loudness * one(*cut)
    return loudness


def centred(key, dims, width, bound, cuts=(), kind=jnp.bfloat16):
    array = jax.random.normal(key, dims, jnp.float32) * width
    if len(cuts) > 0:
        array = steps_of(key, dims, cuts, -0.22, 0.18) * array
    return jnp.clip(array, min=-bound, max=bound).astype(kind)


def setup_inputs(seed: int = 0) -> dict:
    seeds = jax.random.split(jax.random.key(seed), 15)
    return {
        "prompt_query": centred(seeds[0], (GROUPS, PROMPT, HEAD_COUNT * KEY_CHANNELS), 1.0, 6.0, ((0, 8), (1, 4))),
        "prompt_key": centred(seeds[1], (GROUPS, PROMPT, HEAD_COUNT * KEY_CHANNELS), 1.0, 6.0, ((0, 8), (1, 4))),
        "prompt_value": centred(seeds[2], (GROUPS, PROMPT, HEAD_COUNT * DVH), 1.0, 6.0, ((0, 8), (1, 4))),
        "prompt_gate_logit": draw_prompt_gate_logit(jax.random.fold_in(seeds[14], 71), 0),
        "prompt_out_gate": centred(seeds[4], (GROUPS, PROMPT, HEAD_COUNT * DVH), 1.0, 6.0, ((0, 8), (1, 4))),
        "prompt_len": draw_prompt_len(jax.random.fold_in(seeds[14], 71), 0),
        "suffix_query": centred(seeds[6], (REQS, SUFMAX, HEAD_COUNT * KEY_CHANNELS), 1.0, 6.0, ((0, 8),)),
        "suffix_key": centred(seeds[7], (REQS, SUFMAX, HEAD_COUNT * KEY_CHANNELS), 1.0, 6.0, ((0, 8),)),
        "suffix_value": centred(seeds[8], (REQS, SUFMAX, HEAD_COUNT * DVH), 1.0, 6.0, ((0, 8), (2, 4))),
        "suffix_gate_logit": draw_suffix_gate_logit(jax.random.fold_in(seeds[14], 71), 0),
        "suffix_out_gate": centred(seeds[10], (REQS, SUFMAX, HEAD_COUNT * DVH), 1.0, 6.0, ((0, 8), (2, 4))),
        "suffix_len": draw_suffix_len(jax.random.fold_in(seeds[14], 71), 0),
        "request_group": draw_request_group(jax.random.fold_in(seeds[14], 71), 0),
        "norm_gain": jnp.clip(1.0 + 0.18 * jax.random.normal(seeds[13], (DVH,), jnp.float32), 0.1, 1.9),
    }


highest = lax.Precision.HIGHEST
epsilon = 1e-05

def decay_rates(logits):
    return jax.nn.log_sigmoid(logits.astype(jnp.float32)) / 16.0

def block_core(states, queries, key_rows, values, decays):
    running = jnp.cumsum(decays, axis=0)
    closing = running[-1]
    middle = 0.5 * closing
    query_scaled = queries * jnp.exp(running - middle)
    key_scaled = key_rows * jnp.exp(middle - running)
    scores = jnp.einsum('thk,uhk->htu', query_scaled, key_scaled, precision=highest)
    length = queries.shape[0]
    causal = jnp.arange(length, dtype=jnp.int32)[:, None] >= jnp.arange(length, dtype=jnp.int32)[None, :]
    scores = jnp.where(causal[None], scores, 0.0)
    within = jnp.einsum('htu,uhv->thv', scores, values, precision=highest)
    reaching = queries * jnp.exp(running)
    carried = jnp.einsum('thk,khv->thv', reaching, states, precision=highest)
    fading = key_rows * jnp.exp(closing[None] - running)
    updated = jnp.exp(closing).T[:, :, None] * states + jnp.einsum('thk,thv->khv', fading, values, precision=highest)
    return (within + carried, updated, reaching, closing)

def gated_norm(attended, gate_values, gain_row, alive_rows):
    mean_square = lax.optimization_barrier(jnp.mean(attended * attended, axis=-1, keepdims=True))
    normed = attended * lax.rsqrt(mean_square + epsilon) * gain_row
    return normed * gate_values * jax.nn.sigmoid(gate_values) * alive_rows[:, None, None]

def run_carried(start_state, queries, key_rows, values, decays):

    def advance(current, block_input):
        outcome = block_core(current, block_input[0], block_input[1], block_input[2], block_input[3])
        return (outcome[1], outcome[0])
    return lax.scan(advance, start_state, (queries, key_rows, values, decays))

def reference(prompt_query, prompt_key, prompt_value, prompt_gate_logit, prompt_out_gate, prompt_len, suffix_query, suffix_key, suffix_value, suffix_gate_logit, suffix_out_gate, suffix_len, request_group, norm_gain):
    block_count = PROMPT // BL

    def prompt_group(inputs):
        queries, key_rows, values, logits, gate_values, length = inputs
        alive_rows = (jnp.arange(PROMPT, dtype=jnp.int32) < length).astype(jnp.float32)
        mask_rows = alive_rows.reshape(block_count, BL, 1, 1)
        queries = queries.astype(jnp.float32).reshape(block_count, BL, HEAD_COUNT, KEY_CHANNELS) * KEY_CHANNELS ** (-0.5)
        key_rows = key_rows.astype(jnp.float32).reshape(block_count, BL, HEAD_COUNT, KEY_CHANNELS) * mask_rows
        decays = decay_rates(logits).reshape(block_count, BL, HEAD_COUNT, KEY_CHANNELS) * mask_rows
        values = values.astype(jnp.float32).reshape(block_count, BL, HEAD_COUNT, DVH)
        final_state, outputs = run_carried(jnp.zeros((KEY_CHANNELS, HEAD_COUNT, DVH), jnp.float32), queries, key_rows, values, decays)
        outputs = outputs.reshape(PROMPT, HEAD_COUNT, DVH)
        shaped = gated_norm(outputs, gate_values.astype(jnp.float32).reshape(PROMPT, HEAD_COUNT, DVH), norm_gain, alive_rows)
        return (shaped.reshape(PROMPT, HEAD_COUNT * DVH).astype(jnp.bfloat16), final_state)
    prompt_out, finals = lax.map(prompt_group, (prompt_query, prompt_key, prompt_value, prompt_gate_logit, prompt_out_gate, prompt_len))
    suffix_blocks = SUFMAX // BL

    def suffix_request(inputs):
        queries, key_rows, values, logits, gate_values, length, group_index = inputs
        start_state = lax.dynamic_index_in_dim(finals, group_index, 0, keepdims=False)
        alive_rows = (jnp.arange(SUFMAX, dtype=jnp.int32) < length).astype(jnp.float32)
        queries = queries.astype(jnp.float32).reshape(suffix_blocks, BL, HEAD_COUNT, KEY_CHANNELS) * KEY_CHANNELS ** (-0.5)
        key_rows = key_rows.astype(jnp.float32).reshape(suffix_blocks, BL, HEAD_COUNT, KEY_CHANNELS)
        decays = decay_rates(logits).reshape(suffix_blocks, BL, HEAD_COUNT, KEY_CHANNELS)
        values = values.astype(jnp.float32).reshape(suffix_blocks, BL, HEAD_COUNT, DVH)
        ignored_state, outputs = run_carried(start_state, queries, key_rows, values, decays)
        outputs = outputs.reshape(SUFMAX, HEAD_COUNT, DVH)
        shaped = gated_norm(outputs, gate_values.astype(jnp.float32).reshape(SUFMAX, HEAD_COUNT, DVH), norm_gain, alive_rows)
        return shaped.reshape(SUFMAX, HEAD_COUNT * DVH).astype(jnp.bfloat16)
    suffix_out = lax.map(suffix_request, (suffix_query, suffix_key, suffix_value, suffix_gate_logit, suffix_out_gate, suffix_len, request_group))
    return (prompt_out, suffix_out)
```

```python
import functools

import jax
import jax.numpy as jnp
from jax import lax
from jax.experimental import pallas as pl
from jax.experimental.pallas import tpu as pltpu
from jax.sharding import PartitionSpec as P

HEAD_COUNT = 4
KEY_CHANNELS = 256
DVH = 512
CHUNK = 256
HALF = 128
SCALE = KEY_CHANNELS ** (-0.5)
epsilon = 1e-05
f32 = jnp.float32
bf16 = jnp.bfloat16

NN = (((1,), (0,)), ((), ()))
NT = (((1,), (1,)), ((), ()))
TN = (((0,), (0,)), ((), ()))


def dot(a, b, dims):
    return lax.dot_general(a, b, dims, preferred_element_type=f32)


def split(x):
    hi = x.astype(bf16)
    return hi, (x - hi.astype(f32)).astype(bf16)


def dot3(a, b, dims):
    return dot(a[0], b[0], dims) + (dot(a[0], b[1], dims) + dot(a[1], b[0], dims))


def decay_rates(logits):
    x = logits.astype(f32)
    return (jnp.minimum(x, 0.0) - jnp.log(1.0 + jnp.exp(-jnp.abs(x)))) * (1.0 / 16.0)


def running_sum(tri, decay):
    hi = decay.astype(bf16)
    rest = decay - hi.astype(f32)
    mid = rest.astype(bf16)
    low = (rest - mid.astype(f32)).astype(bf16)
    return dot(tri, hi, NN) + (dot(tri, mid, NN) + dot(tri, low, NN))


def column(row):
    turned = jnp.broadcast_to(row, (128, KEY_CHANNELS)).T
    return jnp.concatenate([turned] * (DVH // 128), axis=1)


def alive_column(first, length, rows):
    return (first + lax.broadcasted_iota(jnp.int32, (rows, 1), 0) < length).astype(f32)


def state_kernel(heads, info, k_ref, g_ref, v_ref, s_ref, o_ref):
    j = pl.program_id(1)
    alive = alive_column(info[0] + j * CHUNK, info[1], CHUNK)
    r = lax.broadcasted_iota(jnp.int32, (CHUNK, CHUNK), 0)
    c = lax.broadcasted_iota(jnp.int32, (CHUNK, CHUNK), 1)
    tri = (r >= c).astype(f32).astype(bf16)
    running = running_sum(tri, decay_rates(g_ref[0]) * alive)
    closing = running[CHUNK - 1 :]
    fading = split(k_ref[0].astype(f32) * alive * jnp.exp(closing - running))
    v = v_ref[0]
    update = dot(fading[0], v, TN) + dot(fading[1], v, TN)

    @pl.when(j == 0)
    def _():
        s_ref[0] = update
        o_ref[0] = closing

    @pl.when(j > 0)
    def _():
        s_ref[0] = s_ref[0] * column(jnp.exp(closing)) + update
        o_ref[0] += closing


def chunk_core(q, k, v, decay):
    r = lax.broadcasted_iota(jnp.int32, (CHUNK, CHUNK), 0)
    c = lax.broadcasted_iota(jnp.int32, (CHUNK, CHUNK), 1)
    causal = r >= c
    near = causal & ((r >= HALF) == (c >= HALF))
    running = running_sum(near.astype(f32).astype(bf16), decay)
    half_0 = 0.5 * running[HALF - 1 : HALF]
    half_1 = 0.5 * running[CHUNK - 1 :]
    shift_0 = running[:HALF] - half_0
    shift_1 = running[HALF:] - half_1
    e0, e1 = jnp.exp(half_0), jnp.exp(half_1)
    q0, q1 = q[:HALF] * jnp.exp(shift_0), q[HALF:] * jnp.exp(shift_1)
    k0, k1 = k[:HALF] * jnp.exp(-shift_0), k[HALF:] * jnp.exp(-shift_1)
    reach_1 = q1 * e1
    fade_0 = k0 * e0
    far = dot3(split(reach_1), split(fade_0), NT)
    diag_0 = dot3(split(q0), split(k0), NT)
    diag_1 = dot3(split(q1), split(k1), NT)
    tri = causal[:HALF, :HALF]
    top = jnp.concatenate([jnp.where(tri, diag_0, 0.0), jnp.zeros((HALF, HALF), f32)], axis=1)
    bottom = jnp.concatenate([far, jnp.where(tri, diag_1, 0.0)], axis=1)
    scores = split(jnp.concatenate([top, bottom], axis=0))
    attended = dot(scores[0], v, NN) + dot(scores[1], v, NN)
    reach = jnp.concatenate([q0 * e0, reach_1 * (e0 * e0)], axis=0)
    fade = jnp.concatenate([fade_0 * (e1 * e1), k1 * e1], axis=0)
    return attended, reach, fade, 2.0 * (half_0 + half_1)


def gated(attended, z, gain, alive):
    mean_square = jnp.mean(attended * attended, axis=-1, keepdims=True)
    factor = lax.rsqrt(mean_square * (SCALE * SCALE) + epsilon) * (SCALE * alive)
    z = z.astype(f32)
    return (attended * factor * gain * (z * jax.nn.sigmoid(z))).astype(bf16)


def prompt_kernel(info, q_ref, k_ref, g_ref, v_ref, z_ref, e_ref, gain_ref, out_ref, state):
    j = pl.program_id(1)

    @pl.when(j == 0)
    def _():
        state[...] = e_ref[0]

    alive = alive_column(info[0] + j * CHUNK, info[1], CHUNK)
    v = v_ref[0]
    attended, reach, fade, closing = chunk_core(
        q_ref[0].astype(f32),
        k_ref[0].astype(f32) * alive,
        v,
        decay_rates(g_ref[0]) * alive,
    )
    current = state[...]
    attended += dot3(split(reach), split(current), NN)
    out_ref[0] = gated(attended, z_ref[0], gain_ref[...], alive)

    @pl.when(j < pl.num_programs(1) - 1)
    def _():
        fades = split(fade)
        state[...] = current * column(jnp.exp(closing)) + (dot(fades[0], v, TN) + dot(fades[1], v, TN))


def suffix_local_kernel(head, q_ref, k_ref, g_ref, v_ref, a_ref, r_ref):
    attended, reach, _, _ = chunk_core(
        q_ref[0].astype(f32), k_ref[0].astype(f32), v_ref[0], decay_rates(g_ref[0])
    )
    a_ref[0] = attended
    r_ref[0] = reach


def suffix_final_kernel(group, length, a_ref, r_ref, s_ref, z_ref, gain_ref, out_ref):
    attended = a_ref[0] + dot3(split(r_ref[0]), split(s_ref[0]), NN)
    alive = alive_column(0, length[pl.program_id(0)], CHUNK)
    out_ref[0] = gated(attended, z_ref[0], gain_ref[...], alive)


def cost(flops, data):
    return pl.CostEstimate(flops=int(flops), bytes_accessed=int(data), transcendentals=0)


PARAMS = dict(vmem_limit_bytes=40 << 20)


def local_states(heads, info, k, g, v):
    rows = k.shape[1]
    n = heads.shape[0]
    narrow = pl.BlockSpec((1, CHUNK, KEY_CHANNELS), lambda i, j, heads, info: (0, j, heads[i]))
    wide = pl.BlockSpec((1, CHUNK, DVH), lambda i, j, heads, info: (0, j, heads[i]))
    return pl.pallas_call(
        state_kernel,
        grid_spec=pltpu.PrefetchScalarGridSpec(
            num_scalar_prefetch=2,
            grid=(n, rows // CHUNK),
            in_specs=[narrow, narrow, wide],
            out_specs=[
                pl.BlockSpec((1, KEY_CHANNELS, DVH), lambda i, j, heads, info: (i, 0, 0)),
                pl.BlockSpec((1, 1, KEY_CHANNELS), lambda i, j, heads, info: (i, 0, 0)),
            ],
        ),
        out_shape=[
            jax.ShapeDtypeStruct((n, KEY_CHANNELS, DVH), f32),
            jax.ShapeDtypeStruct((n, 1, KEY_CHANNELS), f32),
        ],
        compiler_params=pltpu.CompilerParams(**PARAMS),
        cost_estimate=cost(4e9, 5e6),
        name="local_states",
    )(heads, info, k, g, v)


def prompt_attention(info, q, k, g, v, z, entering, gain):
    rows = q.shape[1]
    narrow = pl.BlockSpec((1, CHUNK, KEY_CHANNELS), lambda h, j, info: (0, j, h))
    wide = pl.BlockSpec((1, CHUNK, DVH), lambda h, j, info: (0, j, h))
    return pl.pallas_call(
        prompt_kernel,
        grid_spec=pltpu.PrefetchScalarGridSpec(
            num_scalar_prefetch=1,
            grid=(HEAD_COUNT, rows // CHUNK),
            in_specs=[
                narrow,
                narrow,
                narrow,
                wide,
                wide,
                pl.BlockSpec((1, KEY_CHANNELS, DVH), lambda h, j, info: (h, 0, 0)),
                pl.BlockSpec((1, DVH), lambda h, j, info: (0, 0)),
            ],
            out_specs=wide,
            scratch_shapes=[pltpu.VMEM((KEY_CHANNELS, DVH), f32)],
        ),
        out_shape=jax.ShapeDtypeStruct(v.shape, bf16),
        compiler_params=pltpu.CompilerParams(**PARAMS),
        cost_estimate=cost(3e10, 2e7),
        name="prompt_attention",
    )(info, q, k, g, v, z, entering, gain)


def suffix_local(head, q, k, g, v):
    count = q.shape[0]
    narrow = pl.BlockSpec((1, CHUNK, KEY_CHANNELS), lambda i, head: (i, 0, head[0]))
    wide = pl.BlockSpec((1, CHUNK, DVH), lambda i, head: (i, 0, 0))
    return pl.pallas_call(
        suffix_local_kernel,
        grid_spec=pltpu.PrefetchScalarGridSpec(
            num_scalar_prefetch=1,
            grid=(count,),
            in_specs=[narrow, narrow, narrow, wide],
            out_specs=[wide, pl.BlockSpec((1, CHUNK, KEY_CHANNELS), lambda i, head: (i, 0, 0))],
        ),
        out_shape=[
            jax.ShapeDtypeStruct((count, CHUNK, DVH), f32),
            jax.ShapeDtypeStruct((count, CHUNK, KEY_CHANNELS), f32),
        ],
        compiler_params=pltpu.CompilerParams(**PARAMS),
        cost_estimate=cost(6e9, 4e6),
        name="suffix_local",
    )(head, q, k, g, v)


def suffix_final(group, length, attended, reach, finals, z, gain):
    count = attended.shape[0]
    wide = pl.BlockSpec((1, CHUNK, DVH), lambda i, group, length: (i, 0, 0))
    return pl.pallas_call(
        suffix_final_kernel,
        grid_spec=pltpu.PrefetchScalarGridSpec(
            num_scalar_prefetch=2,
            grid=(count,),
            in_specs=[
                wide,
                pl.BlockSpec((1, CHUNK, KEY_CHANNELS), lambda i, group, length: (i, 0, 0)),
                pl.BlockSpec((1, KEY_CHANNELS, DVH), lambda i, group, length: (group[i], 0, 0)),
                wide,
                pl.BlockSpec((1, DVH), lambda i, group, length: (0, 0)),
            ],
            out_specs=wide,
        ),
        out_shape=jax.ShapeDtypeStruct(z.shape, bf16),
        compiler_params=pltpu.CompilerParams(**PARAMS),
        cost_estimate=cost(4e9, 8e6),
        name="suffix_final",
    )(group, length, attended, reach, finals, z, gain)


def fade_state(offset, state):
    return jnp.exp(jnp.swapaxes(offset, -1, -2)) * state


def pick(array, index):
    return lax.dynamic_index_in_dim(array, index, 0, keepdims=False)


def local(
    prompt_query,
    prompt_key,
    prompt_value,
    prompt_gate_logit,
    prompt_out_gate,
    prompt_len,
    suffix_query,
    suffix_key,
    suffix_value,
    suffix_gate_logit,
    suffix_out_gate,
    suffix_len,
    request_group,
    norm_gain,
):
    rank = lax.axis_index("seq")
    side, chip = lax.rem(rank, 2), lax.div(rank, 2)
    rows = prompt_query.shape[1]
    info = jnp.stack([rank * rows, prompt_len[0]]).astype(jnp.int32)
    gain = norm_gain[None]
    both = jnp.arange(2, dtype=jnp.int32) * 2
    across_core = [(0, 1), (1, 0), (2, 3), (3, 2)]
    across_chip = [(0, 2), (1, 3), (2, 0), (3, 1)]

    send_state, send_offset = local_states(
        both + 1 - side, info, prompt_key, prompt_gate_logit, prompt_value
    )
    near_state = lax.ppermute(send_state, "seq", across_core)
    near_offset = lax.ppermute(send_offset, "seq", across_core)
    own_state, own_offset = local_states(
        both + side, info, prompt_key, prompt_gate_logit, prompt_value
    )
    last_offset = jnp.where(side == 0, near_offset, own_offset)
    first_state = jnp.where(side == 0, own_state, near_state)
    last_state = jnp.where(side == 0, near_state, own_state)
    chip_state = fade_state(last_offset, first_state) + last_state
    chip_offset = own_offset + near_offset
    kept_state, kept_offset = pick(chip_state, chip), pick(chip_offset, chip)
    far_state = lax.ppermute(pick(chip_state, 1 - chip), "seq", across_chip)
    far_offset = lax.ppermute(pick(chip_offset, 1 - chip), "seq", across_chip)
    early_state = jnp.where(chip == 0, kept_state, far_state)
    late_state = jnp.where(chip == 0, far_state, kept_state)
    late_offset = jnp.where(chip == 0, far_offset, kept_offset)
    final = fade_state(late_offset, early_state) + late_state
    finals = lax.all_gather(final[None], "req", axis=0, tiled=True)

    suffix_attended, suffix_reach = suffix_local(
        rank.astype(jnp.int32)[None], suffix_query, suffix_key, suffix_gate_logit, suffix_value
    )

    rest = lax.ppermute(kept_state, "seq", [(0, 2), (1, 3)])
    side_heads = jnp.stack([rest, far_state])
    core_heads = lax.ppermute(side_heads, "seq", [(2, 3), (3, 2)])
    core_own = lax.ppermute(own_state, "seq", [(0, 1), (2, 3)])
    second_chip = chip == 1
    second_core = side == 1
    enter_mine = jnp.where(second_chip, side_heads, 0.0)
    enter_other = jnp.where(second_chip, core_heads, 0.0)
    first_other_offset = lax.ppermute(own_offset, "seq", [(0, 1), (2, 3)])
    enter_mine = jnp.where(second_core, fade_state(near_offset, enter_mine) + near_state, enter_mine)
    enter_other = jnp.where(
        second_core, fade_state(first_other_offset, enter_other) + core_own, enter_other
    )
    even = jnp.where(second_core, enter_other, enter_mine)
    odd = jnp.where(second_core, enter_mine, enter_other)
    entering = jnp.stack([even, odd], axis=1).reshape(HEAD_COUNT, KEY_CHANNELS, DVH)
    prompt_result = prompt_attention(
        info,
        prompt_query,
        prompt_key,
        prompt_gate_logit,
        prompt_value,
        prompt_out_gate,
        entering,
        gain,
    )
    suffix_result = suffix_final(
        request_group, suffix_len, suffix_attended, suffix_reach, finals, suffix_out_gate, gain
    )
    return (prompt_result, suffix_result)


def solution(mesh):
    placed = (
        P("req", "seq", None),
        P("req", "seq", None),
        P("req", "seq", None),
        P("req", "seq", None),
        P("req", "seq", None),
        P("req"),
        P("req", None, None),
        P("req", None, None),
        P("req", None, "seq"),
        P("req", None, None),
        P("req", None, "seq"),
        P("req"),
        P("req"),
        P(),
    )
    return jax.shard_map(
        local,
        mesh=mesh,
        in_specs=placed,
        out_specs=(P("req", "seq", None), P("req", None, "seq")),
        check_vma=False,
    )
```

```python
import functools

import jax
import jax.numpy as jnp
from jax import lax
from jax.experimental import pallas as pl
from jax.experimental.pallas import tpu as pltpu
from jax.sharding import PartitionSpec as P

HEAD_COUNT = 4
KEY_CHANNELS = 256
DVH = 512
CHUNK = 256
HALF = 128
SCALE = KEY_CHANNELS ** (-0.5)
epsilon = 1e-05
f32 = jnp.float32
bf16 = jnp.bfloat16

NN = (((1,), (0,)), ((), ()))
NT = (((1,), (1,)), ((), ()))
TN = (((0,), (0,)), ((), ()))


def dot(a, b, dims):
    return lax.dot_general(a, b, dims, preferred_element_type=f32)


def split(x):
    hi = x.astype(bf16)
    return hi, (x - hi.astype(f32)).astype(bf16)


def dot3(a, b, dims):
    return dot(a[0], b[0], dims) + (dot(a[0], b[1], dims) + dot(a[1], b[0], dims))


def decay_rates(logits):
    x = logits.astype(f32)
    return (jnp.minimum(x, 0.0) - jnp.log(1.0 + jnp.exp(-jnp.abs(x)))) * (1.0 / 16.0)


def running_sum(tri, decay):
    hi, lo = split(decay)
    return dot(tri, hi, NN) + dot(tri, lo, NN)


def column(row):
    turned = jnp.broadcast_to(row, (128, KEY_CHANNELS)).T
    return jnp.concatenate([turned] * (DVH // 128), axis=1)


def alive_column(first, length, rows):
    return (first + lax.broadcasted_iota(jnp.int32, (rows, 1), 0) < length).astype(f32)


def state_kernel(heads, info, k_ref, g_ref, v_ref, s_ref, o_ref):
    rows = k_ref.shape[1]
    r = lax.broadcasted_iota(jnp.int32, (CHUNK, CHUNK), 0)
    c = lax.broadcasted_iota(jnp.int32, (CHUNK, CHUNK), 1)
    later = (r < c).astype(f32).astype(bf16)
    after = jnp.zeros((1, KEY_CHANNELS), f32)
    highs, lows = [], []
    for j in reversed(range(rows // CHUNK)):
        span = pl.ds(j * CHUNK, CHUNK)
        alive = alive_column(info[0] + j * CHUNK, info[1], CHUNK)
        decay = decay_rates(g_ref[0, span]) * alive
        to_end = running_sum(later, decay)
        high, low = split(k_ref[0, span].astype(f32) * alive * jnp.exp(to_end + after))
        highs.insert(0, high)
        lows.insert(0, low)
        after += to_end[:1] + decay[:1]
    v = v_ref[0]
    s_ref[0] = dot(jnp.concatenate(highs, axis=0), v, TN) + dot(jnp.concatenate(lows, axis=0), v, TN)
    o_ref[0] = after


def chunk_core(q, k, v, decay):
    r = lax.broadcasted_iota(jnp.int32, (CHUNK, CHUNK), 0)
    c = lax.broadcasted_iota(jnp.int32, (CHUNK, CHUNK), 1)
    causal = r >= c
    near = causal & ((r >= HALF) == (c >= HALF))
    running = running_sum(near.astype(f32).astype(bf16), decay)
    half_0 = 0.5 * running[HALF - 1 : HALF]
    half_1 = 0.5 * running[CHUNK - 1 :]
    shift_0 = running[:HALF] - half_0
    shift_1 = running[HALF:] - half_1
    e0, e1 = jnp.exp(half_0), jnp.exp(half_1)
    q0, q1 = q[:HALF] * jnp.exp(shift_0), q[HALF:] * jnp.exp(shift_1)
    k0, k1 = k[:HALF] * jnp.exp(-shift_0), k[HALF:] * jnp.exp(-shift_1)
    reach_1 = q1 * e1
    fade_0 = k0 * e0
    far = dot3(split(reach_1), split(fade_0), NT)
    diag_0 = dot3(split(q0), split(k0), NT)
    diag_1 = dot3(split(q1), split(k1), NT)
    tri = causal[:HALF, :HALF]
    top = jnp.concatenate([jnp.where(tri, diag_0, 0.0), jnp.zeros((HALF, HALF), f32)], axis=1)
    bottom = jnp.concatenate([far, jnp.where(tri, diag_1, 0.0)], axis=1)
    scores = split(jnp.concatenate([top, bottom], axis=0))
    attended = dot(scores[0], v, NN) + dot(scores[1], v, NN)
    reach = jnp.concatenate([q0 * e0, reach_1 * (e0 * e0)], axis=0)
    fade = jnp.concatenate([fade_0 * (e1 * e1), k1 * e1], axis=0)
    return attended, reach, fade, 2.0 * (half_0 + half_1)


def gated(attended, z, gain, alive):
    mean_square = jnp.mean(attended * attended, axis=-1, keepdims=True)
    factor = lax.rsqrt(mean_square * (SCALE * SCALE) + epsilon) * (SCALE * alive)
    z = z.astype(f32)
    return (attended * factor * gain * (z * jax.nn.sigmoid(z))).astype(bf16)


def prompt_kernel(info, q_ref, k_ref, g_ref, v_ref, z_ref, e_ref, gain_ref, out_ref, state):
    j = pl.program_id(1)

    @pl.when(j == 0)
    def _():
        state[...] = e_ref[0]

    alive = alive_column(info[0] + j * CHUNK, info[1], CHUNK)
    v = v_ref[0]
    attended, reach, fade, closing = chunk_core(
        q_ref[0].astype(f32),
        k_ref[0].astype(f32) * alive,
        v,
        decay_rates(g_ref[0]) * alive,
    )
    current = state[...]
    attended += dot3(split(reach), split(current), NN)
    out_ref[0] = gated(attended, z_ref[0], gain_ref[...], alive)

    @pl.when(j < pl.num_programs(1) - 1)
    def _():
        fades = split(fade)
        state[...] = current * column(jnp.exp(closing)) + (dot(fades[0], v, TN) + dot(fades[1], v, TN))


def suffix_local_kernel(head, q_ref, k_ref, g_ref, v_ref, a_ref, r_ref):
    attended, reach, _, _ = chunk_core(
        q_ref[0].astype(f32), k_ref[0].astype(f32), v_ref[0], decay_rates(g_ref[0])
    )
    a_ref[0] = attended
    r_ref[0] = reach


def suffix_final_kernel(group, length, a_ref, r_ref, s_ref, z_ref, gain_ref, out_ref):
    attended = a_ref[0] + dot3(split(r_ref[0]), split(s_ref[0]), NN)
    alive = alive_column(0, length[pl.program_id(0)], CHUNK)
    out_ref[0] = gated(attended, z_ref[0], gain_ref[...], alive)


def cost(flops, data):
    return pl.CostEstimate(flops=int(flops), bytes_accessed=int(data), transcendentals=0)


PARAMS = dict(vmem_limit_bytes=60 << 20)


def local_states(heads, info, k, g, v):
    rows = k.shape[1]
    n = heads.shape[0]
    narrow = pl.BlockSpec((1, rows, KEY_CHANNELS), lambda i, heads, info: (0, 0, heads[i]))
    wide = pl.BlockSpec((1, rows, DVH), lambda i, heads, info: (0, 0, heads[i]))
    return pl.pallas_call(
        state_kernel,
        grid_spec=pltpu.PrefetchScalarGridSpec(
            num_scalar_prefetch=2,
            grid=(n,),
            in_specs=[narrow, narrow, wide],
            out_specs=[
                pl.BlockSpec((1, KEY_CHANNELS, DVH), lambda i, heads, info: (i, 0, 0)),
                pl.BlockSpec((1, 1, KEY_CHANNELS), lambda i, heads, info: (i, 0, 0)),
            ],
        ),
        out_shape=[
            jax.ShapeDtypeStruct((n, KEY_CHANNELS, DVH), f32),
            jax.ShapeDtypeStruct((n, 1, KEY_CHANNELS), f32),
        ],
        compiler_params=pltpu.CompilerParams(**PARAMS),
        cost_estimate=cost(4e9, 5e6),
        name="local_states",
    )(heads, info, k, g, v)


def prompt_attention(info, q, k, g, v, z, entering, gain):
    rows = q.shape[1]
    narrow = pl.BlockSpec((1, CHUNK, KEY_CHANNELS), lambda h, j, info: (0, j, h))
    wide = pl.BlockSpec((1, CHUNK, DVH), lambda h, j, info: (0, j, h))
    return pl.pallas_call(
        prompt_kernel,
        grid_spec=pltpu.PrefetchScalarGridSpec(
            num_scalar_prefetch=1,
            grid=(HEAD_COUNT, rows // CHUNK),
            in_specs=[
                narrow,
                narrow,
                narrow,
                wide,
                wide,
                pl.BlockSpec((1, KEY_CHANNELS, DVH), lambda h, j, info: (h, 0, 0)),
                pl.BlockSpec((1, DVH), lambda h, j, info: (0, 0)),
            ],
            out_specs=wide,
            scratch_shapes=[pltpu.VMEM((KEY_CHANNELS, DVH), f32)],
        ),
        out_shape=jax.ShapeDtypeStruct(v.shape, bf16),
        compiler_params=pltpu.CompilerParams(**PARAMS),
        cost_estimate=cost(3e10, 2e7),
        name="prompt_attention",
    )(info, q, k, g, v, z, entering, gain)


def suffix_local(head, q, k, g, v):
    count = q.shape[0]
    narrow = pl.BlockSpec((1, CHUNK, KEY_CHANNELS), lambda i, head: (i, 0, head[0]))
    wide = pl.BlockSpec((1, CHUNK, DVH), lambda i, head: (i, 0, 0))
    return pl.pallas_call(
        suffix_local_kernel,
        grid_spec=pltpu.PrefetchScalarGridSpec(
            num_scalar_prefetch=1,
            grid=(count,),
            in_specs=[narrow, narrow, narrow, wide],
            out_specs=[wide, pl.BlockSpec((1, CHUNK, KEY_CHANNELS), lambda i, head: (i, 0, 0))],
        ),
        out_shape=[
            jax.ShapeDtypeStruct((count, CHUNK, DVH), f32),
            jax.ShapeDtypeStruct((count, CHUNK, KEY_CHANNELS), f32),
        ],
        compiler_params=pltpu.CompilerParams(**PARAMS),
        cost_estimate=cost(6e9, 4e6),
        name="suffix_local",
    )(head, q, k, g, v)


def suffix_final(group, length, attended, reach, finals, z, gain):
    count = attended.shape[0]
    wide = pl.BlockSpec((1, CHUNK, DVH), lambda i, group, length: (i, 0, 0))
    return pl.pallas_call(
        suffix_final_kernel,
        grid_spec=pltpu.PrefetchScalarGridSpec(
            num_scalar_prefetch=2,
            grid=(count,),
            in_specs=[
                wide,
                pl.BlockSpec((1, CHUNK, KEY_CHANNELS), lambda i, group, length: (i, 0, 0)),
                pl.BlockSpec((1, KEY_CHANNELS, DVH), lambda i, group, length: (group[i], 0, 0)),
                wide,
                pl.BlockSpec((1, DVH), lambda i, group, length: (0, 0)),
            ],
            out_specs=wide,
        ),
        out_shape=jax.ShapeDtypeStruct(z.shape, bf16),
        compiler_params=pltpu.CompilerParams(**PARAMS),
        cost_estimate=cost(4e9, 8e6),
        name="suffix_final",
    )(group, length, attended, reach, finals, z, gain)


def fade_state(offset, state):
    return jnp.exp(jnp.swapaxes(offset, -1, -2)) * state


def pick(array, index):
    return lax.dynamic_index_in_dim(array, index, 0, keepdims=False)


def local(
    prompt_query,
    prompt_key,
    prompt_value,
    prompt_gate_logit,
    prompt_out_gate,
    prompt_len,
    suffix_query,
    suffix_key,
    suffix_value,
    suffix_gate_logit,
    suffix_out_gate,
    suffix_len,
    request_group,
    norm_gain,
):
    rank = lax.axis_index("seq")
    side, chip = lax.rem(rank, 2), lax.div(rank, 2)
    rows = prompt_query.shape[1]
    info = jnp.stack([rank * rows, prompt_len[0]]).astype(jnp.int32)
    gain = norm_gain[None]
    both = jnp.arange(2, dtype=jnp.int32) * 2
    across_core = [(0, 1), (1, 0), (2, 3), (3, 2)]
    across_chip = [(0, 2), (1, 3), (2, 0), (3, 1)]

    send_state, send_offset = local_states(
        both + 1 - side, info, prompt_key, prompt_gate_logit, prompt_value
    )
    near_state = lax.ppermute(send_state, "seq", across_core)
    near_offset = lax.ppermute(send_offset, "seq", across_core)
    own_state, own_offset = local_states(
        both + side, info, prompt_key, prompt_gate_logit, prompt_value
    )
    last_offset = jnp.where(side == 0, near_offset, own_offset)
    first_state = jnp.where(side == 0, own_state, near_state)
    last_state = jnp.where(side == 0, near_state, own_state)
    chip_state = fade_state(last_offset, first_state) + last_state
    chip_offset = own_offset + near_offset
    kept_state, kept_offset = pick(chip_state, chip), pick(chip_offset, chip)
    far_state = lax.ppermute(pick(chip_state, 1 - chip), "seq", across_chip)
    far_offset = lax.ppermute(pick(chip_offset, 1 - chip), "seq", across_chip)
    early_state = jnp.where(chip == 0, kept_state, far_state)
    late_state = jnp.where(chip == 0, far_state, kept_state)
    late_offset = jnp.where(chip == 0, far_offset, kept_offset)
    final = fade_state(late_offset, early_state) + late_state
    finals = lax.all_gather(final[None], "req", axis=0, tiled=True)

    suffix_attended, suffix_reach = suffix_local(
        rank.astype(jnp.int32)[None], suffix_query, suffix_key, suffix_gate_logit, suffix_value
    )

    rest = lax.ppermute(kept_state, "seq", [(0, 2), (1, 3)])
    side_heads = jnp.stack([rest, far_state])
    core_heads = lax.ppermute(side_heads, "seq", [(2, 3), (3, 2)])
    core_own = lax.ppermute(own_state, "seq", [(0, 1), (2, 3)])
    second_chip = chip == 1
    second_core = side == 1
    enter_mine = jnp.where(second_chip, side_heads, 0.0)
    enter_other = jnp.where(second_chip, core_heads, 0.0)
    first_other_offset = lax.ppermute(own_offset, "seq", [(0, 1), (2, 3)])
    enter_mine = jnp.where(second_core, fade_state(near_offset, enter_mine) + near_state, enter_mine)
    enter_other = jnp.where(
        second_core, fade_state(first_other_offset, enter_other) + core_own, enter_other
    )
    even = jnp.where(second_core, enter_other, enter_mine)
    odd = jnp.where(second_core, enter_mine, enter_other)
    entering = jnp.stack([even, odd], axis=1).reshape(HEAD_COUNT, KEY_CHANNELS, DVH)
    prompt_result = prompt_attention(
        info,
        prompt_query,
        prompt_key,
        prompt_gate_logit,
        prompt_value,
        prompt_out_gate,
        entering,
        gain,
    )
    suffix_result = suffix_final(
        request_group, suffix_len, suffix_attended, suffix_reach, finals, suffix_out_gate, gain
    )
    return (prompt_result, suffix_result)


def solution(mesh):
    placed = (
        P("req", "seq", None),
        P("req", "seq", None),
        P("req", "seq", None),
        P("req", "seq", None),
        P("req", "seq", None),
        P("req"),
        P("req", None, None),
        P("req", None, None),
        P("req", None, "seq"),
        P("req", None, None),
        P("req", None, "seq"),
        P("req"),
        P("req"),
        P(),
    )
    return jax.shard_map(
        local,
        mesh=mesh,
        in_specs=placed,
        out_specs=(P("req", "seq", None), P("req", None, "seq")),
        check_vma=False,
    )
```

```python
import functools

import jax
import jax.numpy as jnp
from jax import lax
from jax.experimental import pallas as pl
from jax.experimental.pallas import tpu as pltpu
from jax.sharding import PartitionSpec as P

HEAD_COUNT = 4
KEY_CHANNELS = 256
DVH = 512
CHUNK = 256
HALF = 128
SCALE = KEY_CHANNELS ** (-0.5)
epsilon = 1e-05
f32 = jnp.float32
bf16 = jnp.bfloat16

NN = (((1,), (0,)), ((), ()))
NT = (((1,), (1,)), ((), ()))
TN = (((0,), (0,)), ((), ()))


def dot(a, b, dims):
    return lax.dot_general(a, b, dims, preferred_element_type=f32)


def split(x):
    hi = x.astype(bf16)
    return hi, (x - hi.astype(f32)).astype(bf16)


def dot3(a, b, dims):
    return dot(a[0], b[0], dims) + (dot(a[0], b[1], dims) + dot(a[1], b[0], dims))


def decay_rates(logits):
    x = logits.astype(f32)
    return (jnp.minimum(x, 0.0) - jnp.log(1.0 + jnp.exp(-jnp.abs(x)))) * (1.0 / 16.0)


def running_sum(tri, decay):
    hi, lo = split(decay)
    return dot(tri, hi, NN) + dot(tri, lo, NN)


def column(row):
    turned = jnp.broadcast_to(row, (128, KEY_CHANNELS)).T
    return jnp.concatenate([turned] * (DVH // 128), axis=1)


def alive_column(first, length, rows):
    return (first + lax.broadcasted_iota(jnp.int32, (rows, 1), 0) < length).astype(f32)


def state_kernel(heads, info, k_ref, g_ref, v_ref, s_ref, o_ref):
    rows = k_ref.shape[1]
    r = lax.broadcasted_iota(jnp.int32, (CHUNK, CHUNK), 0)
    c = lax.broadcasted_iota(jnp.int32, (CHUNK, CHUNK), 1)
    later = (r < c).astype(f32).astype(bf16)
    after = jnp.zeros((1, KEY_CHANNELS), f32)
    highs, lows = [], []
    for j in reversed(range(rows // CHUNK)):
        span = pl.ds(j * CHUNK, CHUNK)
        alive = alive_column(info[0] + j * CHUNK, info[1], CHUNK)
        decay = decay_rates(g_ref[0, span]) * alive
        to_end = running_sum(later, decay)
        high, low = split(k_ref[0, span].astype(f32) * alive * jnp.exp(to_end + after))
        highs.insert(0, high)
        lows.insert(0, low)
        after += to_end[:1] + decay[:1]
    v = v_ref[0]
    s_ref[0] = dot(jnp.concatenate(highs, axis=0), v, TN) + dot(jnp.concatenate(lows, axis=0), v, TN)
    o_ref[0] = after


def chunk_core(q, k, v, decay):
    r = lax.broadcasted_iota(jnp.int32, (CHUNK, CHUNK), 0)
    c = lax.broadcasted_iota(jnp.int32, (CHUNK, CHUNK), 1)
    causal = r >= c
    near = causal & ((r >= HALF) == (c >= HALF))
    running = running_sum(near.astype(f32).astype(bf16), decay)
    half_0 = 0.5 * running[HALF - 1 : HALF]
    half_1 = 0.5 * running[CHUNK - 1 :]
    shift_0 = running[:HALF] - half_0
    shift_1 = running[HALF:] - half_1
    e0, e1 = jnp.exp(half_0), jnp.exp(half_1)
    q0, q1 = q[:HALF] * jnp.exp(shift_0), q[HALF:] * jnp.exp(shift_1)
    k0, k1 = k[:HALF] * jnp.exp(-shift_0), k[HALF:] * jnp.exp(-shift_1)
    reach_1 = q1 * e1
    fade_0 = k0 * e0
    far = dot3(split(reach_1), split(fade_0), NT)
    diag_0 = dot3(split(q0), split(k0), NT)
    diag_1 = dot3(split(q1), split(k1), NT)
    tri = causal[:HALF, :HALF]
    top = jnp.concatenate([jnp.where(tri, diag_0, 0.0), jnp.zeros((HALF, HALF), f32)], axis=1)
    bottom = jnp.concatenate([far, jnp.where(tri, diag_1, 0.0)], axis=1)
    scores = split(jnp.concatenate([top, bottom], axis=0))
    attended = dot(scores[0], v, NN) + dot(scores[1], v, NN)
    reach = jnp.concatenate([q0 * e0, reach_1 * (e0 * e0)], axis=0)
    fade = jnp.concatenate([fade_0 * (e1 * e1), k1 * e1], axis=0)
    return attended, reach, fade, 2.0 * (half_0 + half_1)


def gated(attended, z, gain, alive):
    mean_square = jnp.mean(attended * attended, axis=-1, keepdims=True)
    factor = lax.rsqrt(mean_square * (SCALE * SCALE) + epsilon) * (SCALE * alive)
    z = z.astype(f32)
    return (attended * factor * gain * (z * jax.nn.sigmoid(z))).astype(bf16)


def prompt_kernel(info, q_ref, k_ref, g_ref, v_ref, z_ref, e_ref, gain_ref, out_ref, state):
    j = pl.program_id(1)

    @pl.when(j == 0)
    def _():
        state[...] = e_ref[0]

    alive = alive_column(info[0] + j * CHUNK, info[1], CHUNK)
    v = v_ref[0]
    attended, reach, fade, closing = chunk_core(
        q_ref[0].astype(f32),
        k_ref[0].astype(f32) * alive,
        v,
        decay_rates(g_ref[0]) * alive,
    )
    current = state[...]
    attended += dot3(split(reach), split(current), NN)
    out_ref[0] = gated(attended, z_ref[0], gain_ref[...], alive)

    @pl.when(j < pl.num_programs(1) - 1)
    def _():
        fades = split(fade)
        state[...] = current * column(jnp.exp(closing)) + (dot(fades[0], v, TN) + dot(fades[1], v, TN))


def suffix_local_kernel(head, q_ref, k_ref, g_ref, v_ref, a_ref, r_ref):
    attended, reach, _, _ = chunk_core(
        q_ref[0].astype(f32), k_ref[0].astype(f32), v_ref[0], decay_rates(g_ref[0])
    )
    a_ref[0] = attended
    r_ref[0] = reach


def suffix_final_kernel(group, slot, length, a_ref, r_ref, s_ref, t_ref, z_ref, gain_ref, out_ref):
    attended = a_ref[0] + dot3(
        split(r_ref[0]), split(jnp.concatenate([s_ref[0], t_ref[0]], axis=1)), NN
    )
    alive = alive_column(0, length[pl.program_id(0)], CHUNK)
    out_ref[0] = gated(attended, z_ref[0], gain_ref[...], alive)


def cost(flops, data):
    return pl.CostEstimate(flops=int(flops), bytes_accessed=int(data), transcendentals=0)


PARAMS = dict(vmem_limit_bytes=60 << 20)


def local_states(heads, info, k, g, v):
    rows = k.shape[1]
    n = heads.shape[0]
    narrow = pl.BlockSpec((1, rows, KEY_CHANNELS), lambda i, heads, info: (0, 0, heads[i]))
    wide = pl.BlockSpec((1, rows, DVH), lambda i, heads, info: (0, 0, heads[i]))
    return pl.pallas_call(
        state_kernel,
        grid_spec=pltpu.PrefetchScalarGridSpec(
            num_scalar_prefetch=2,
            grid=(n,),
            in_specs=[narrow, narrow, wide],
            out_specs=[
                pl.BlockSpec((1, KEY_CHANNELS, DVH), lambda i, heads, info: (i, 0, 0)),
                pl.BlockSpec((1, 1, KEY_CHANNELS), lambda i, heads, info: (i, 0, 0)),
            ],
        ),
        out_shape=[
            jax.ShapeDtypeStruct((n, KEY_CHANNELS, DVH), f32),
            jax.ShapeDtypeStruct((n, 1, KEY_CHANNELS), f32),
        ],
        compiler_params=pltpu.CompilerParams(**PARAMS),
        cost_estimate=cost(4e9, 5e6),
        name="local_states",
    )(heads, info, k, g, v)


def prompt_attention(info, q, k, g, v, z, entering, gain):
    rows = q.shape[1]
    narrow = pl.BlockSpec((1, CHUNK, KEY_CHANNELS), lambda h, j, info: (0, j, h))
    wide = pl.BlockSpec((1, CHUNK, DVH), lambda h, j, info: (0, j, h))
    return pl.pallas_call(
        prompt_kernel,
        grid_spec=pltpu.PrefetchScalarGridSpec(
            num_scalar_prefetch=1,
            grid=(HEAD_COUNT, rows // CHUNK),
            in_specs=[
                narrow,
                narrow,
                narrow,
                wide,
                wide,
                pl.BlockSpec((1, KEY_CHANNELS, DVH), lambda h, j, info: (h, 0, 0)),
                pl.BlockSpec((1, DVH), lambda h, j, info: (0, 0)),
            ],
            out_specs=wide,
            scratch_shapes=[pltpu.VMEM((KEY_CHANNELS, DVH), f32)],
        ),
        out_shape=jax.ShapeDtypeStruct(v.shape, bf16),
        compiler_params=pltpu.CompilerParams(**PARAMS),
        cost_estimate=cost(3e10, 2e7),
        name="prompt_attention",
    )(info, q, k, g, v, z, entering, gain)


def suffix_local(head, q, k, g, v):
    count = q.shape[0]
    narrow = pl.BlockSpec((1, CHUNK, KEY_CHANNELS), lambda i, head: (i, 0, head[0]))
    wide = pl.BlockSpec((1, CHUNK, DVH), lambda i, head: (i, 0, 0))
    return pl.pallas_call(
        suffix_local_kernel,
        grid_spec=pltpu.PrefetchScalarGridSpec(
            num_scalar_prefetch=1,
            grid=(count,),
            in_specs=[narrow, narrow, narrow, wide],
            out_specs=[wide, pl.BlockSpec((1, CHUNK, KEY_CHANNELS), lambda i, head: (i, 0, 0))],
        ),
        out_shape=[
            jax.ShapeDtypeStruct((count, CHUNK, DVH), f32),
            jax.ShapeDtypeStruct((count, CHUNK, KEY_CHANNELS), f32),
        ],
        compiler_params=pltpu.CompilerParams(**PARAMS),
        cost_estimate=cost(6e9, 4e6),
        name="suffix_local",
    )(head, q, k, g, v)


def suffix_final(group, slot, length, attended, reach, finals, others, z, gain):
    count = attended.shape[0]
    wide = pl.BlockSpec((1, CHUNK, DVH), lambda i, group, slot, length: (i, 0, 0))
    return pl.pallas_call(
        suffix_final_kernel,
        grid_spec=pltpu.PrefetchScalarGridSpec(
            num_scalar_prefetch=3,
            grid=(count,),
            in_specs=[
                wide,
                pl.BlockSpec((1, CHUNK, KEY_CHANNELS), lambda i, group, slot, length: (i, 0, 0)),
                pl.BlockSpec((1, KEY_CHANNELS, DVH // 2), lambda i, group, slot, length: (group[i], 0, 0)),
                pl.BlockSpec((1, KEY_CHANNELS, DVH // 2), lambda i, group, slot, length: (slot[i], 0, 0)),
                wide,
                pl.BlockSpec((1, DVH), lambda i, group, slot, length: (0, 0)),
            ],
            out_specs=wide,
        ),
        out_shape=jax.ShapeDtypeStruct(z.shape, bf16),
        compiler_params=pltpu.CompilerParams(**PARAMS),
        cost_estimate=cost(4e9, 8e6),
        name="suffix_final",
    )(group, slot, length, attended, reach, finals, others, z, gain)


def gather_by_permutes(part, group):
    def shift(value, step, sources):
        return lax.ppermute(value, "req", [(2 * z + y, 2 * (z + step) + y) for z in sources for y in (0, 1)])

    up, down = [part], [part]
    for k in (1, 2, 3):
        up.append(shift(up[-1], 1, range(k - 1, 3)))
        down.append(shift(down[-1], -1, range(1, 5 - k)))
    along = [part] + [up[k] + down[4 - k] for k in (1, 2, 3)]
    swap = [(i, i ^ 1) for i in range(8)]
    slots = [x for value in along for x in (value, lax.ppermute(value, "req", swap))]
    me = lax.axis_index("req")
    behind = lax.rem(me // 2 - group // 2 + 4, 4)
    return jnp.stack(slots), 2 * behind + jnp.abs(lax.rem(me, 2) - lax.rem(group, 2))


def fade_state(offset, state):
    return jnp.exp(jnp.swapaxes(offset, -1, -2)) * state


def pick(array, index):
    return lax.dynamic_index_in_dim(array, index, 0, keepdims=False)


def local(
    prompt_query,
    prompt_key,
    prompt_value,
    prompt_gate_logit,
    prompt_out_gate,
    prompt_len,
    suffix_query,
    suffix_key,
    suffix_value,
    suffix_gate_logit,
    suffix_out_gate,
    suffix_len,
    request_group,
    norm_gain,
):
    rank = lax.axis_index("seq")
    side, chip = lax.rem(rank, 2), lax.div(rank, 2)
    rows = prompt_query.shape[1]
    info = jnp.stack([rank * rows, prompt_len[0]]).astype(jnp.int32)
    gain = norm_gain[None]
    both = jnp.arange(2, dtype=jnp.int32) * 2
    across_core = [(0, 1), (1, 0), (2, 3), (3, 2)]
    across_chip = [(0, 2), (1, 3), (2, 0), (3, 1)]

    send_state, send_offset = local_states(
        both + 1 - side, info, prompt_key, prompt_gate_logit, prompt_value
    )
    near_state = lax.ppermute(send_state, "seq", across_core)
    near_offset = lax.ppermute(send_offset, "seq", across_core)
    own_state, own_offset = local_states(
        both + side, info, prompt_key, prompt_gate_logit, prompt_value
    )
    last_offset = jnp.where(side == 0, near_offset, own_offset)
    first_state = jnp.where(side == 0, own_state, near_state)
    last_state = jnp.where(side == 0, near_state, own_state)
    chip_state = fade_state(last_offset, first_state) + last_state
    chip_offset = own_offset + near_offset
    kept_state, kept_offset = pick(chip_state, chip), pick(chip_offset, chip)
    far_state = lax.ppermute(pick(chip_state, 1 - chip), "seq", across_chip)
    far_offset = lax.ppermute(pick(chip_offset, 1 - chip), "seq", across_chip)
    early_state = jnp.where(chip == 0, kept_state, far_state)
    late_state = jnp.where(chip == 0, far_state, kept_state)
    late_offset = jnp.where(chip == 0, far_offset, kept_offset)
    final = fade_state(late_offset, early_state) + late_state
    half = DVH // 2
    finals = lax.all_gather(final[None, :, :half], "req", axis=0, tiled=True)
    if lax.axis_size("req") == 8:
        others, slot = gather_by_permutes(final[:, half:], request_group)
    else:
        others = lax.all_gather(final[None, :, half:], "req", axis=0, tiled=True)
        slot = request_group

    suffix_attended, suffix_reach = suffix_local(
        rank.astype(jnp.int32)[None], suffix_query, suffix_key, suffix_gate_logit, suffix_value
    )

    rest = lax.ppermute(kept_state, "seq", [(0, 2), (1, 3)])
    side_heads = jnp.stack([rest, far_state])
    core_heads = lax.ppermute(side_heads, "seq", [(2, 3), (3, 2)])
    core_own = lax.ppermute(own_state, "seq", [(0, 1), (2, 3)])
    second_chip = chip == 1
    second_core = side == 1
    enter_mine = jnp.where(second_chip, side_heads, 0.0)
    enter_other = jnp.where(second_chip, core_heads, 0.0)
    first_other_offset = lax.ppermute(own_offset, "seq", [(0, 1), (2, 3)])
    enter_mine = jnp.where(second_core, fade_state(near_offset, enter_mine) + near_state, enter_mine)
    enter_other = jnp.where(
        second_core, fade_state(first_other_offset, enter_other) + core_own, enter_other
    )
    even = jnp.where(second_core, enter_other, enter_mine)
    odd = jnp.where(second_core, enter_mine, enter_other)
    entering = jnp.stack([even, odd], axis=1).reshape(HEAD_COUNT, KEY_CHANNELS, DVH)
    prompt_result = prompt_attention(
        info,
        prompt_query,
        prompt_key,
        prompt_gate_logit,
        prompt_value,
        prompt_out_gate,
        entering,
        gain,
    )
    suffix_result = suffix_final(
        request_group, slot, suffix_len, suffix_attended, suffix_reach, finals, others, suffix_out_gate, gain
    )
    return (prompt_result, suffix_result)


def solution(mesh):
    placed = (
        P("req", "seq", None),
        P("req", "seq", None),
        P("req", "seq", None),
        P("req", "seq", None),
        P("req", "seq", None),
        P("req"),
        P("req", None, None),
        P("req", None, None),
        P("req", None, "seq"),
        P("req", None, None),
        P("req", None, "seq"),
        P("req"),
        P("req"),
        P(),
    )
    return jax.shard_map(
        local,
        mesh=mesh,
        in_specs=placed,
        out_specs=(P("req", "seq", None), P("req", None, "seq")),
        check_vma=False,
    )
```
